32 devices in a mesh: pole: 4 (over y, x), node: 8 (over z, core).
Axes of the slice: x: 2, y: 2, z: 4, core: 2. Of those that a mesh axis runs over, the one named last changes fastest.
Arguments:
- dens_part: bfloat16 [4, 32768, 338], P('pole', 'node'), may hold values from -1.5 to 1.5
- dest_node: int32 [32768], P('node'), may hold values from 0 to 7, as said below
- pair_slot: int32 [32768], P('node'), may hold values from 0 to 1023, as said below
- deriv: bfloat16 [32768, 1014], P(('pole', 'node')), may hold values from -0.119628906 to 0.119628906
- pair_atoms: int32 [2, 32768], P(None, ('pole', 'node')), may hold values from 0 to 4095
Outputs:
- forces: float32 [3, 4096], P(None, ('pole', 'node'))
The draws below stay inside these ranges and needn't reach their ends.
Inputs may be any that keep to these rules, and one draw needn't show every extreme that they name: The share of block s is (s // 1024) % 4. Of the 1024 blocks of one share at most 256 have the same dest_node, and in every share exactly 256 do for some node index. Within one pole index, the number of blocks that a share on node n sends to node (n + k) % 8 depends on k alone. Every pair of pole index p and node index m receives exactly 1024 blocks of share p. `pair_slot`: the blocks of share p with dest_node m take each position of 0 to 1023 exactly once.
All inputs are finite; a program needn't handle non-finite values.
Results may differ from the reference program's by a relative error of at most 0.009.
Values may be sent and summed in bfloat16 or wider, within the bound.
A program may use at most 64 MiB of HBM per device.

```python
import jax
import jax.numpy as jnp
from jax import lax

BSQ = 169
BLK_DEV = 1024
NB = 32768
ATOMS = 4096
CAP = 256
N_POLE = 4
N_NODE = 8


def routing(key):
    base_key = jax.random.fold_in(key, 7)
    k_off, k_cnt, k_send, k_recv = jax.random.split(base_key, 4)
    half_cap = CAP // 2
    offsets = jax.vmap(lambda subkey: jax.random.permutation(subkey, N_NODE)[:N_NODE - 1])(jax.random.split(k_off, N_POLE))
    pair_count = (N_NODE - 2) // 2
    spread = jax.random.randint(k_cnt, (N_POLE, pair_count), -(half_cap - 1), half_cap)
    counts = jnp.concatenate([jnp.full((N_POLE, 1), CAP, jnp.int32), half_cap + spread, half_cap - spread], axis=1).astype(jnp.int32)
    starts = jnp.cumsum(counts, axis=1) - counts
    position = jnp.arange(BLK_DEV, dtype=jnp.int32)
    run_index = jnp.sum((position[None, :, None] >= starts[:, None, 1:]).astype(jnp.int32), axis=2)
    offset_of = jnp.take_along_axis(offsets.astype(jnp.int32), run_index, axis=1)
    send_order = jax.vmap(lambda subkey: jax.random.permutation(subkey, BLK_DEV))(jax.random.split(k_send, N_POLE * N_NODE)).reshape(N_POLE, N_NODE, BLK_DEV).astype(jnp.int32)
    recv_order = jax.vmap(lambda subkey: jax.random.permutation(subkey, BLK_DEV))(jax.random.split(k_recv, N_POLE * N_NODE)).reshape(N_POLE, N_NODE, BLK_DEV).astype(jnp.int32)
    node_index = jnp.arange(N_NODE, dtype=jnp.int32)[None, :, None]
    pole_index = jnp.arange(N_POLE, dtype=jnp.int32)[:, None, None]
    offset_block = offset_of[pole_index, send_order]
    target_node = (node_index + offset_block) % N_NODE
    target_slot = recv_order[pole_index, target_node, send_order]
    target_node = jnp.transpose(target_node, (1, 0, 2)).reshape(-1).astype(jnp.int32)
    target_slot = jnp.transpose(target_slot, (1, 0, 2)).reshape(-1).astype(jnp.int32)
    return (target_node, target_slot)


def draw_dest_node(key, part):
    return routing(key)[0]


def draw_pair_slot(key, part):
    return routing(key)[1]


def touch_ends(drawn, stream_key, smallest, top_value):
    dims = drawn.shape
    place = [jax.random.randint(jax.random.fold_in(stream_key, axis), (), 0, dims[axis]) for axis in range(len(dims))]
    drawn = drawn.at[tuple(place)].set(smallest)
    longest = dims.index(max(dims))
    place[longest] = (place[longest] + 1) % dims[longest]
    return drawn.at[tuple(place)].set(top_value)


def block_scale(own_key, shape, shards, low, top_value):
    def one(dim, blocks):
        heights = jax.random.uniform(jax.random.fold_in(jax.random.fold_in(own_key, 6), dim), (blocks,), jnp.float32, low / len(shards), top_value / len(shards))
        return jnp.repeat(jnp.exp(heights), shape[dim] // blocks).reshape((-1,) + (1,) * (len(shape) - dim - 1))

    factor_of = one(*shards[0])
    for cut in shards[1:]:
        factor_of = factor_of * one(*cut)
    return factor_of


def noise(key, dims, width, reach, cuts=(), kind=jnp.bfloat16):
    drawn = jax.random.normal(key, dims, jnp.float32) * width
    if len(cuts) > 0:
        drawn = block_scale(key, dims, cuts, -0.22, 0.18) * drawn
    return jnp.clip(drawn, min=-reach, max=reach).astype(kind)


def setup_inputs(seed: int = 0) -> dict:
    streams_of = jax.random.split(jax.random.key(seed), 6)
    dens_part = noise(streams_of[0], (N_POLE, NB, 2 * BSQ), 0.25, 1.5, ((0, 4), (1, 8)))
    dest_node = draw_dest_node(jax.random.fold_in(streams_of[5], 71), 0)
    pair_slot = draw_pair_slot(jax.random.fold_in(streams_of[5], 71), 0)
    deriv = noise(streams_of[3], (NB, 6 * BSQ), 0.02, 0.119628906, ((0, 32),))
    pair_atoms = touch_ends(jax.random.randint(streams_of[4], (2, NB), 0, ATOMS), jax.random.fold_in(streams_of[4], 1), 0, ATOMS - 1).astype(jnp.int32)
    return dict(dens_part=dens_part, dest_node=dest_node, pair_slot=pair_slot, deriv=deriv, pair_atoms=pair_atoms)


def contract_tile(tiles):
    density_tile, deriv_tile = tiles
    density_tile = density_tile.astype(jnp.float32)
    deriv_tile = deriv_tile.astype(jnp.float32)
    grad_h = deriv_tile[:, : 3 * BSQ].reshape(-1, 3, BSQ)
    grad_s = deriv_tile[:, 3 * BSQ:].reshape(-1, 3, BSQ)
    first = jnp.einsum("bk,bck->bc", density_tile[:, :BSQ], grad_h, precision=lax.Precision.HIGHEST)
    second = jnp.einsum("bk,bck->bc", density_tile[:, BSQ:], grad_s, precision=lax.Precision.HIGHEST)
    return first - second


def reference(dens_part, dest_node, pair_slot, deriv, pair_atoms):
    summed = jnp.sum(dens_part.astype(jnp.float32), axis=0).astype(jnp.bfloat16)
    block_index = jnp.arange(NB, dtype=jnp.int32)
    share_index = (block_index // BLK_DEV) % N_POLE
    target = ((share_index * N_NODE + dest_node) * BLK_DEV + pair_slot).astype(jnp.int32)
    pair_dens = jnp.zeros_like(summed).at[target].set(summed)
    groups = NB // BLK_DEV
    pair_term = lax.map(contract_tile, (pair_dens.reshape(groups, BLK_DEV, 2 * BSQ), deriv.reshape(groups, BLK_DEV, 6 * BSQ)))
    pair_term = pair_term.reshape(NB, 3)
    forces_out = jnp.zeros((3, ATOMS), jnp.float32)
    forces_out = forces_out.at[:, pair_atoms[0]].add(-2.0 * pair_term.T)
    forces_out = forces_out.at[:, pair_atoms[1]].add(2.0 * pair_term.T)
    return forces_out
```

```python
import functools

import jax
import jax.numpy as jnp
from jax import lax
from jax.experimental import pallas as pl
from jax.experimental.pallas import tpu as pltpu
from jax.sharding import PartitionSpec as P

LANES = 128
CHUNK = 128
ROWS = 8
DIGIT = 32
MESH = pl.DeviceIdType.MESH
NT = (((1,), (1,)), ((), ()))
F32 = jnp.float32
BF16 = jnp.bfloat16


def iota(shape, dim):
    return lax.broadcasted_iota(jnp.int32, shape, dim)


def onehot(cond):
    return jnp.where(cond, 1.0, 0.0).astype(BF16)


def split_two(x):
    high = x.astype(BF16)
    return high, (x - high.astype(F32)).astype(BF16)


def kernel(
    poles, nodes, blocks, width, cap,
    dens, node_ref, slot_ref, deriv, atoms, out,
    own, parts, dv, aligned, pack, place, ranks, slot_rows, slot_send, slot_recv,
    send_buf, recv_buf, density, acc, force, force_in, force_two, force_last,
    own_sem, dv_sem, rs_send, rs_recv, sl_send, sl_recv, ex_send, ex_recv,
    fa_send, fa_recv, fb_send, fb_recv,
):
    half = width // 2
    chunks = -(-width // CHUNK)
    total = deriv.shape[0]
    pole = lax.axis_index("pole")
    node = lax.axis_index("node")

    def near_first(i):
        return nodes // 2 + (1 - 2 * (i % 2)) * ((i + 1) // 2)

    def rows(t):
        return min(CHUNK, width - t * CHUNK)

    own_copies = []
    for t in range(chunks):
        copy = pltpu.make_async_copy(
            dens.at[pl.ds(t * CHUNK, rows(t)), pl.ds(pole * blocks, blocks)],
            own[t],
            own_sem.at[t],
        )
        own_copies.append(copy)
    dv_copy = pltpu.make_async_copy(deriv, dv, dv_sem)

    barrier = pltpu.get_barrier_semaphore()
    for r in range(1, poles):
        pl.semaphore_signal(
            barrier, inc=1, device_id={"pole": (pole + r) % poles}, device_id_type=MESH
        )

    @pl.loop(1, nodes)
    def _(k):
        pl.semaphore_signal(
            barrier, inc=1, device_id={"node": (node + k) % nodes}, device_id_type=MESH
        )

    for copy in own_copies:
        copy.start()
    dv_copy.start()
    pl.semaphore_wait(barrier, poles - 1 + nodes - 1)

    def rs_copy(t, r):
        dest = (pole + r) % poles
        return pltpu.make_async_remote_copy(
            src_ref=dens.at[pl.ds(t * CHUNK, rows(t)), pl.ds(dest * blocks, blocks)],
            dst_ref=parts[t].at[r - 1],
            send_sem=rs_send.at[t, r - 1],
            recv_sem=rs_recv.at[t, r - 1],
            device_id={"pole": dest},
            device_id_type=MESH,
        )

    for t in range(chunks):
        for r in range(1, poles):
            rs_copy(t, r).start()

    dest_row = node_ref[pl.ds(pole, 1), :]
    slot_row = slot_ref[pl.ds(pole, 1), :]
    hot = dest_row == iota((nodes, blocks), 0)
    before = onehot(iota((blocks, blocks), 0) < iota((blocks, blocks), 1))
    rank = jnp.dot(onehot(hot), before, preferred_element_type=F32)
    ranks[...] = jnp.where(hot, rank, -1.0)
    digit_high = (slot_row // DIGIT + 1).astype(F32)
    digit_low = (slot_row % DIGIT).astype(F32)
    which = iota((ROWS, blocks), 0)
    slot_rows[...] = jnp.where(
        which == 0, digit_high, jnp.where(which == 1, digit_low, 0.0)
    ).astype(BF16)

    def slot_copy(k):
        return pltpu.make_async_remote_copy(
            src_ref=slot_send.at[k],
            dst_ref=slot_recv.at[k],
            send_sem=sl_send.at[k],
            recv_sem=sl_recv.at[k],
            device_id={"node": (node + k) % nodes},
            device_id_type=MESH,
        )

    def make_pack(k):
        row = ranks[pl.ds((node + k) % nodes, 1), :]
        pack[k] = onehot(row == iota((cap, blocks), 0).astype(F32))
        return lax.dot_general(slot_rows[...], pack[k], NT, preferred_element_type=F32)

    @pl.loop(1, nodes)
    def _(k):
        slot_send[k] = make_pack(k)
        slot_copy(k).start()

    slot_recv[0] = make_pack(0)

    dv_copy.wait()
    wide = chunks * CHUNK
    for c in range(3):
        for start, first, sign in ((c * half, 0, 1.0), ((3 + c) * half, half, -1.0)):
            low = start // LANES * LANES
            high = min(-(-(start + half) // LANES) * LANES, total)
            src = iota((wide, high - low), 1) + (low - start)
            row = iota((wide, high - low), 0) - first
            moved = jnp.where((src == row) & (row >= 0) & (row < half), sign, 0.0).astype(BF16)
            piece = jnp.dot(moved, dv[low:high, :], preferred_element_type=F32)
            got = piece if first == 0 else got + piece
        aligned[c] = got.astype(BF16)

    def ex_copy(t, k):
        return pltpu.make_async_remote_copy(
            src_ref=send_buf[t].at[k],
            dst_ref=recv_buf[t].at[k],
            send_sem=ex_send.at[t, k],
            recv_sem=ex_recv.at[t, k],
            device_id={"node": (node + k) % nodes},
            device_id_type=MESH,
        )

    def exchange(t):
        own_copies[t].wait()
        for r in range(1, poles):
            rs_copy(t, r).wait_recv()
        summed = own[t][...].astype(F32)
        for r in range(1, poles):
            summed = summed + parts[t][r - 1].astype(F32)
        density[t][...] = summed.astype(BF16)

        def packed(k):
            return lax.dot_general(
                density[t][...], pack[k], NT, preferred_element_type=F32
            ).astype(BF16)

        @pl.loop(0, nodes - 1)
        def _(i):
            k = near_first(i)
            send_buf[t][k] = packed(k)
            ex_copy(t, k).start()

        recv_buf[t][0] = packed(0)

    def make_place(k):
        digits = slot_recv[k]
        slot = (digits[0:1, :] - 1.0) * DIGIT + digits[1:2, :]
        place[k] = onehot(slot == iota((blocks, cap), 0).astype(F32))

    def contract(t):
        def placed(k):
            return lax.dot_general(
                recv_buf[t][k], place[k], NT, preferred_element_type=F32
            )

        acc[t][...] = placed(0)

        @pl.loop(0, nodes - 1)
        def _(i):
            k = near_first(nodes - 2 - i)
            ex_copy(t, k).wait_recv()
            acc[t][...] += placed(k)

        sums = jnp.zeros((ROWS, blocks), F32)
        for c in range(3):
            prod = acc[t][...] * aligned[c, t * CHUNK:t * CHUNK + rows(t), :].astype(F32)
            sums = jnp.where(which == c, jnp.sum(prod, axis=0, keepdims=True), sums)
        return sums

    exchange(0)
    make_place(0)

    @pl.loop(1, nodes)
    def _(k):
        slot_copy(k).wait_recv()
        make_place(k)

    term = None
    for t in range(1, chunks):
        exchange(t)
        part = contract(t - 1)
        term = part if term is None else term + part
    part = contract(chunks - 1)
    term = part if term is None else term + part

    owners = poles * nodes
    group = min(owners, 32)
    height = group * ROWS
    pieces = split_two(2.0 * term)
    for g in range(owners // group):
        block = iota((height, blocks), 0) // ROWS + g * group
        owner = (block % poles) * nodes + block // poles
        result = None
        for end in range(2):
            atom = atoms[end:end + 1, :]
            low = onehot(atom % LANES == iota((LANES, blocks), 0))
            here = (atom // LANES) == owner
            for piece in pieces:
                value = jnp.tile(piece.astype(F32), (group, 1))
                lhs = jnp.where(here, value if end == 1 else -value, 0.0).astype(BF16)
                got = lax.dot_general(lhs, low, NT, preferred_element_type=F32)
                result = got if result is None else result + got
        span = group // poles
        force[g * span:(g + 1) * span] = result.reshape(span, poles, ROWS, LANES)

    def fa_copy(k):
        dest = (node + k) % nodes
        return pltpu.make_async_remote_copy(
            src_ref=force.at[dest],
            dst_ref=force_in.at[k],
            send_sem=fa_send.at[k],
            recv_sem=fa_recv.at[k],
            device_id={"node": dest},
            device_id_type=MESH,
        )

    @pl.loop(0, nodes - 1)
    def _(i):
        fa_copy(near_first(i)).start()

    force_two[...] = force[node]

    @pl.loop(0, nodes - 1)
    def _(i):
        k = near_first(nodes - 2 - i)
        fa_copy(k).wait_recv()
        force_two[...] += force_in[k]

    def fb_copy(r):
        dest = (pole + r) % poles
        return pltpu.make_async_remote_copy(
            src_ref=force_two.at[dest],
            dst_ref=force_last.at[r],
            send_sem=fb_send.at[r],
            recv_sem=fb_recv.at[r],
            device_id={"pole": dest},
            device_id_type=MESH,
        )

    for r in range(1, poles):
        fb_copy(r).start()
    final = force_two[pole]
    for r in range(1, poles):
        fb_copy(r).wait_recv()
        final = final + force_last[r]
    out[...] = final[0:3, :]

    for t in range(chunks):
        for r in range(1, poles):
            rs_copy(t, r).wait_send()

        @pl.loop(1, nodes)
        def _(k):
            ex_copy(t, k).wait_send()

    @pl.loop(1, nodes)
    def _(k):
        slot_copy(k).wait_send()
        fa_copy(k).wait_send()

    for r in range(1, poles):
        fb_copy(r).wait_send()


def body(dens_part, dest_node, pair_slot, deriv, pair_atoms):
    blocks = deriv.shape[0]
    total = deriv.shape[1]
    width = dens_part.shape[2]
    nodes = lax.axis_size("node")
    poles = lax.axis_size("pole")
    cap = 2 * blocks // nodes
    chunks = -(-width // CHUNK)
    sizes = [min(CHUNK, width - t * CHUNK) for t in range(chunks)]
    dma = pltpu.SemaphoreType.DMA
    vmem = pl.BlockSpec(memory_space=pltpu.VMEM)
    hbm = pl.BlockSpec(memory_space=pl.ANY)
    return pl.pallas_call(
        functools.partial(kernel, poles, nodes, blocks, width, cap),
        out_shape=jax.ShapeDtypeStruct((3, LANES), F32),
        in_specs=[hbm, vmem, vmem, hbm, vmem],
        out_specs=vmem,
        scratch_shapes=[
            [pltpu.VMEM((n, blocks), BF16) for n in sizes],
            [pltpu.VMEM((poles - 1, n, blocks), BF16) for n in sizes],
            pltpu.VMEM((total, blocks), BF16),
            pltpu.VMEM((3, chunks * CHUNK, blocks), BF16),
            pltpu.VMEM((nodes, cap, blocks), BF16),
            pltpu.VMEM((nodes, blocks, cap), BF16),
            pltpu.VMEM((nodes, blocks), F32),
            pltpu.VMEM((ROWS, blocks), BF16),
            pltpu.VMEM((nodes, ROWS, cap), F32),
            pltpu.VMEM((nodes, ROWS, cap), F32),
            [pltpu.VMEM((nodes, n, cap), BF16) for n in sizes],
            [pltpu.VMEM((nodes, n, cap), BF16) for n in sizes],
            [pltpu.VMEM((n, blocks), BF16) for n in sizes],
            [pltpu.VMEM((n, blocks), F32) for n in sizes],
            pltpu.VMEM((nodes, poles, ROWS, LANES), F32),
            pltpu.VMEM((nodes, poles, ROWS, LANES), F32),
            pltpu.VMEM((poles, ROWS, LANES), F32),
            pltpu.VMEM((poles, ROWS, LANES), F32),
            dma((chunks,)),
            dma,
            dma((chunks, poles - 1)),
            dma((chunks, poles - 1)),
            dma((nodes,)),
            dma((nodes,)),
            dma((chunks, nodes)),
            dma((chunks, nodes)),
            dma((nodes,)),
            dma((nodes,)),
            dma((poles,)),
            dma((poles,)),
        ],
        compiler_params=pltpu.CompilerParams(
            collective_id=0, has_side_effects=True, vmem_limit_bytes=60 << 20
        ),
    )(
        dens_part[0].T,
        dest_node.reshape(poles, blocks),
        pair_slot.reshape(poles, blocks),
        deriv.T,
        pair_atoms,
    )


def solution(mesh):
    return jax.shard_map(
        body,
        mesh=mesh,
        in_specs=(
            P("pole", "node", None),
            P("node"),
            P("node"),
            P(("pole", "node"), None),
            P(None, ("pole", "node")),
        ),
        out_specs=P(None, ("pole", "node")),
        check_vma=False,
    )
```

```python
import functools

import jax
import jax.numpy as jnp
from jax import lax
from jax.experimental import pallas as pl
from jax.experimental.pallas import tpu as pltpu
from jax.sharding import PartitionSpec as P

LANES = 128
CHUNK = 96
ROWS = 8
DIGIT = 32
PART = 4
MESH = pl.DeviceIdType.MESH
NT = (((1,), (1,)), ((), ()))
F32 = jnp.float32
BF16 = jnp.bfloat16


def iota(shape, dim):
    return lax.broadcasted_iota(jnp.int32, shape, dim)


def onehot(cond):
    return jnp.where(cond, 1.0, 0.0).astype(BF16)


def split_two(x):
    high = x.astype(BF16)
    return high, (x - high.astype(F32)).astype(BF16)


def kernel(
    poles, nodes, blocks, width, cap,
    dens, node_hbm, slot_hbm, deriv, atoms, out,
    own, parts, dv, aligned, pack, place, ranks, slot_rows, slot_send, slot_recv,
    send_buf, recv_buf, density, acc, force, force_in, force_two, force_last,
    own_sem, dv_sem, rs_send, rs_recv, sl_send, sl_recv, ex_send, ex_recv,
    fa_send, fa_recv, fb_send, fb_recv, node_ref, slot_ref, int_sem,
):
    half = width // 2
    chunks = -(-width // CHUNK)
    total = deriv.shape[0]
    pole = lax.axis_index("pole")
    node = lax.axis_index("node")

    def near_first(i):
        return nodes // 2 + (1 - 2 * (i % 2)) * ((i + 1) // 2)

    def rows(t):
        return min(CHUNK, width - t * CHUNK)

    own_copies = []
    for t in range(chunks):
        copy = pltpu.make_async_copy(
            dens.at[pl.ds(t * CHUNK, rows(t)), pl.ds(pole * blocks, blocks)],
            own[t],
            own_sem.at[t],
        )
        own_copies.append(copy)
    int_copies = [
        pltpu.make_async_copy(ref.at[pl.ds(pole * blocks, blocks)], row.at[0], int_sem.at[i])
        for i, (ref, row) in enumerate(((node_hbm, node_ref), (slot_hbm, slot_ref)))
    ]
    dv_copy = pltpu.make_async_copy(deriv, dv, dv_sem)

    barrier = pltpu.get_barrier_semaphore()
    for r in range(1, poles):
        pl.semaphore_signal(
            barrier, inc=1, device_id={"pole": (pole + r) % poles}, device_id_type=MESH
        )

    @pl.loop(1, nodes)
    def _(k):
        pl.semaphore_signal(
            barrier, inc=1, device_id={"node": (node + k) % nodes}, device_id_type=MESH
        )

    for copy in int_copies + own_copies:
        copy.start()
    dv_copy.start()
    pl.semaphore_wait(barrier, poles - 1 + nodes - 1)

    def rs_copy(t, r):
        dest = (pole + r) % poles
        return pltpu.make_async_remote_copy(
            src_ref=dens.at[pl.ds(t * CHUNK, rows(t)), pl.ds(dest * blocks, blocks)],
            dst_ref=parts[t].at[r - 1],
            send_sem=rs_send.at[t, r - 1],
            recv_sem=rs_recv.at[t, r - 1],
            device_id={"pole": dest},
            device_id_type=MESH,
        )

    for t in range(chunks):
        for r in range(1, poles):
            rs_copy(t, r).start()

    for copy in int_copies:
        copy.wait()
    dest_row = node_ref[...]
    slot_row = slot_ref[...]
    hot = dest_row == iota((nodes, blocks), 0)
    before = onehot(iota((blocks, blocks), 0) < iota((blocks, blocks), 1))
    rank = jnp.dot(onehot(hot), before, preferred_element_type=F32)
    ranks[...] = jnp.where(hot, rank, -1.0)
    digit_high = (slot_row // DIGIT + 1).astype(F32)
    digit_low = (slot_row % DIGIT).astype(F32)
    which = iota((ROWS, blocks), 0)
    slot_rows[...] = jnp.where(
        which == 0, digit_high, jnp.where(which == 1, digit_low, 0.0)
    ).astype(BF16)

    def slot_copy(k):
        return pltpu.make_async_remote_copy(
            src_ref=slot_send.at[k],
            dst_ref=slot_recv.at[k],
            send_sem=sl_send.at[k],
            recv_sem=sl_recv.at[k],
            device_id={"node": (node + k) % nodes},
            device_id_type=MESH,
        )

    def make_pack(k):
        row = ranks[pl.ds((node + k) % nodes, 1), :]
        pack[k] = onehot(row == iota((cap, blocks), 0).astype(F32))
        return lax.dot_general(slot_rows[...], pack[k], NT, preferred_element_type=F32)

    @pl.loop(1, nodes)
    def _(k):
        slot_send[k] = make_pack(k)
        slot_copy(k).start()

    slot_recv[0] = make_pack(0)

    dv_copy.wait()
    wide = chunks * CHUNK
    for c in range(3):
        for start, first, sign in ((c * half, 0, 1.0), ((3 + c) * half, half, -1.0)):
            low = start // LANES * LANES
            high = min(-(-(start + half) // LANES) * LANES, total)
            src = iota((wide, high - low), 1) + (low - start)
            row = iota((wide, high - low), 0) - first
            moved = jnp.where((src == row) & (row >= 0) & (row < half), sign, 0.0).astype(BF16)
            piece = jnp.dot(moved, dv[low:high, :], preferred_element_type=F32)
            got = piece if first == 0 else got + piece
        aligned[c] = got.astype(BF16)

    def ex_copy(t, k):
        return pltpu.make_async_remote_copy(
            src_ref=send_buf[t].at[k],
            dst_ref=recv_buf[t].at[k],
            send_sem=ex_send.at[t, k],
            recv_sem=ex_recv.at[t, k],
            device_id={"node": (node + k) % nodes},
            device_id_type=MESH,
        )

    def exchange(t):
        own_copies[t].wait()
        for r in range(1, poles):
            rs_copy(t, r).wait_recv()
        summed = own[t][...].astype(F32)
        for r in range(1, poles):
            summed = summed + parts[t][r - 1].astype(F32)
        density[t][...] = summed.astype(BF16)

        def packed(k):
            return lax.dot_general(
                density[t][...], pack[k], NT, preferred_element_type=F32
            ).astype(BF16)

        @pl.loop(0, nodes - 1)
        def _(i):
            k = near_first(i)
            send_buf[t][k] = packed(k)
            ex_copy(t, k).start()

        recv_buf[t][0] = packed(0)

    def make_place(k):
        digits = slot_recv[k]
        slot = (digits[0:1, :] - 1.0) * DIGIT + digits[1:2, :]
        place[k] = onehot(slot == iota((blocks, cap), 0).astype(F32))

    def contract(t):
        def placed(k):
            return lax.dot_general(
                recv_buf[t][k], place[k], NT, preferred_element_type=F32
            )

        acc[t][...] = placed(0)

        @pl.loop(0, nodes - 1)
        def _(i):
            k = near_first(nodes - 2 - i)
            ex_copy(t, k).wait_recv()
            acc[t][...] += placed(k)

        sums = jnp.zeros((ROWS, blocks), F32)
        for c in range(3):
            prod = acc[t][...] * aligned[c, t * CHUNK:t * CHUNK + rows(t), :].astype(F32)
            sums = jnp.where(which % PART == c, jnp.sum(prod, axis=0, keepdims=True), sums)
        return sums

    exchange(0)
    make_place(0)

    @pl.loop(1, nodes)
    def _(k):
        slot_copy(k).wait_recv()
        make_place(k)

    term = None
    for t in range(1, chunks):
        exchange(t)
        part = contract(t - 1)
        term = part if term is None else term + part
    part = contract(chunks - 1)
    term = part if term is None else term + part

    owners = poles * nodes
    group = min(owners, 32)
    height = group * PART
    pieces = split_two(2.0 * term)
    for g in range(owners // group):
        block = iota((height, blocks), 0) // PART + g * group
        owner = (block % poles) * nodes + block // poles
        result = None
        for end in range(2):
            atom = atoms[end:end + 1, :]
            low = onehot(atom % LANES == iota((LANES, blocks), 0))
            here = (atom // LANES) == owner
            for piece in pieces:
                value = jnp.tile(piece.astype(F32), (group // 2, 1))
                lhs = jnp.where(here, value if end == 1 else -value, 0.0).astype(BF16)
                got = lax.dot_general(lhs, low, NT, preferred_element_type=F32)
                result = got if result is None else result + got
        span = group // poles
        force[g * span:(g + 1) * span] = result.reshape(span, poles // 2, ROWS, LANES)

    def fa_copy(k):
        dest = (node + k) % nodes
        return pltpu.make_async_remote_copy(
            src_ref=force.at[dest],
            dst_ref=force_in.at[k],
            send_sem=fa_send.at[k],
            recv_sem=fa_recv.at[k],
            device_id={"node": dest},
            device_id_type=MESH,
        )

    @pl.loop(0, nodes - 1)
    def _(i):
        fa_copy(near_first(i)).start()

    force_two[...] = force[node]

    @pl.loop(0, nodes - 1)
    def _(i):
        k = near_first(nodes - 2 - i)
        fa_copy(k).wait_recv()
        force_two[...] += force_in[k]

    def fb_copy(r):
        dest = (pole + r) % poles
        return pltpu.make_async_remote_copy(
            src_ref=force_two.at[dest // 2],
            dst_ref=force_last.at[r],
            send_sem=fb_send.at[r],
            recv_sem=fb_recv.at[r],
            device_id={"pole": dest},
            device_id_type=MESH,
        )

    for r in range(1, poles):
        fb_copy(r).start()
    final = force_two[pole // 2]
    for r in range(1, poles):
        fb_copy(r).wait_recv()
        final = final + force_last[r]
    out[...] = jnp.where(pole % 2 == 0, final[0:3, :], final[PART:PART + 3, :])

    for t in range(chunks):
        for r in range(1, poles):
            rs_copy(t, r).wait_send()

        @pl.loop(1, nodes)
        def _(k):
            ex_copy(t, k).wait_send()

    @pl.loop(1, nodes)
    def _(k):
        slot_copy(k).wait_send()
        fa_copy(k).wait_send()

    for r in range(1, poles):
        fb_copy(r).wait_send()


def body(dens_part, dest_node, pair_slot, deriv, pair_atoms):
    blocks = deriv.shape[0]
    total = deriv.shape[1]
    width = dens_part.shape[2]
    nodes = lax.axis_size("node")
    poles = lax.axis_size("pole")
    cap = 2 * blocks // nodes
    chunks = -(-width // CHUNK)
    sizes = [min(CHUNK, width - t * CHUNK) for t in range(chunks)]
    dma = pltpu.SemaphoreType.DMA
    vmem = pl.BlockSpec(memory_space=pltpu.VMEM)
    hbm = pl.BlockSpec(memory_space=pl.ANY)
    return pl.pallas_call(
        functools.partial(kernel, poles, nodes, blocks, width, cap),
        out_shape=jax.ShapeDtypeStruct((3, LANES), F32),
        in_specs=[hbm, hbm, hbm, hbm, vmem],
        out_specs=vmem,
        scratch_shapes=[
            [pltpu.VMEM((n, blocks), BF16) for n in sizes],
            [pltpu.VMEM((poles - 1, n, blocks), BF16) for n in sizes],
            pltpu.VMEM((total, blocks), BF16),
            pltpu.VMEM((3, chunks * CHUNK, blocks), BF16),
            pltpu.VMEM((nodes, cap, blocks), BF16),
            pltpu.VMEM((nodes, blocks, cap), BF16),
            pltpu.VMEM((nodes, blocks), F32),
            pltpu.VMEM((ROWS, blocks), BF16),
            pltpu.VMEM((nodes, ROWS, cap), F32),
            pltpu.VMEM((nodes, ROWS, cap), F32),
            [pltpu.VMEM((nodes, n, cap), BF16) for n in sizes],
            [pltpu.VMEM((nodes, n, cap), BF16) for n in sizes],
            [pltpu.VMEM((n, blocks), BF16) for n in sizes],
            [pltpu.VMEM((n, blocks), F32) for n in sizes],
            pltpu.VMEM((nodes, poles // 2, ROWS, LANES), F32),
            pltpu.VMEM((nodes, poles // 2, ROWS, LANES), F32),
            pltpu.VMEM((poles // 2, ROWS, LANES), F32),
            pltpu.VMEM((poles, ROWS, LANES), F32),
            dma((chunks,)),
            dma,
            dma((chunks, poles - 1)),
            dma((chunks, poles - 1)),
            dma((nodes,)),
            dma((nodes,)),
            dma((chunks, nodes)),
            dma((chunks, nodes)),
            dma((nodes,)),
            dma((nodes,)),
            dma((poles,)),
            dma((poles,)),
            pltpu.VMEM((1, blocks), jnp.int32),
            pltpu.VMEM((1, blocks), jnp.int32),
            dma((2,)),
        ],
        compiler_params=pltpu.CompilerParams(
            collective_id=0, has_side_effects=True, vmem_limit_bytes=60 << 20
        ),
    )(
        dens_part[0].T,
        dest_node,
        pair_slot,
        deriv.T,
        pair_atoms,
    )


def solution(mesh):
    return jax.shard_map(
        body,
        mesh=mesh,
        in_specs=(
            P("pole", "node", None),
            P("node"),
            P("node"),
            P(("pole", "node"), None),
            P(None, ("pole", "node")),
        ),
        out_specs=P(None, ("pole", "node")),
        check_vma=False,
    )
```

```python
import functools

import jax
import jax.numpy as jnp
from jax import lax
from jax.experimental import pallas as pl
from jax.experimental.pallas import tpu as pltpu
from jax.sharding import PartitionSpec as P

LANES = 128
CHUNK = 96
ROWS = 8
DIGIT = 32
PART = 4
MESH = pl.DeviceIdType.MESH
NT = (((1,), (1,)), ((), ()))
F32 = jnp.float32
BF16 = jnp.bfloat16


def iota(shape, dim):
    return lax.broadcasted_iota(jnp.int32, shape, dim)


def onehot(cond):
    return jnp.where(cond, 1.0, 0.0).astype(BF16)


def split_two(x):
    high = x.astype(BF16)
    return high, (x - high.astype(F32)).astype(BF16)


def kernel(
    poles, nodes, blocks, width, cap,
    dens, node_hbm, slot_hbm, deriv, atoms, out,
    own, first_in, mid, second_in, dv, aligned, pack, place, ranks, slot_rows, slot_send, slot_recv,
    send_buf, recv_buf, density, acc, force, force_in, force_two, force_last,
    own_sem, dv_sem, one_send, one_recv, two_send, two_recv, sl_send, sl_recv, ex_send, ex_recv,
    fa_send, fa_recv, fb_send, fb_recv, node_ref, slot_ref, int_sem,
):
    half = width // 2
    chunks = -(-width // CHUNK)
    total = deriv.shape[0]
    pole = lax.axis_index("pole")
    node = lax.axis_index("node")

    def near_first(i):
        return nodes // 2 + (1 - 2 * (i % 2)) * ((i + 1) // 2)

    def rows(t):
        return min(CHUNK, width - t * CHUNK)

    digits = (pole % 2, pole // 2)

    def index(stripe, first, second):
        return second * 2 + first if stripe == 0 else first * 2 + second

    def stripe_rows(t, stripe):
        top = rows(t) // 2 // 16 * 16
        return (0, top) if stripe == 0 else (top, rows(t) - top)

    def source(t, stripe, share):
        start, size = stripe_rows(t, stripe)
        return dens.at[pl.ds(t * CHUNK + start, size), pl.ds(share * blocks, blocks)]

    def own_copy(t, stripe, e):
        return pltpu.make_async_copy(
            source(t, stripe, index(stripe, digits[stripe], e)),
            own[t][stripe].at[e],
            own_sem.at[t, stripe, e],
        )

    def one_copy(t, stripe, e):
        there = 1 - digits[stripe]
        return pltpu.make_async_remote_copy(
            src_ref=source(t, stripe, index(stripe, there, e)),
            dst_ref=first_in[t][stripe].at[e],
            send_sem=one_send.at[t, stripe, e],
            recv_sem=one_recv.at[t, stripe, e],
            device_id={"pole": index(stripe, there, digits[1 - stripe])},
            device_id_type=MESH,
        )

    def two_copy(t, stripe):
        return pltpu.make_async_remote_copy(
            src_ref=mid[t][stripe],
            dst_ref=second_in[t][stripe],
            send_sem=two_send.at[t, stripe],
            recv_sem=two_recv.at[t, stripe],
            device_id={"pole": index(stripe, digits[stripe], 1 - digits[1 - stripe])},
            device_id_type=MESH,
        )

    def start_one(t):
        if t < chunks:
            for e in (1, 0):
                for stripe in range(2):
                    mine = digits[1 - stripe]
                    one_copy(t, stripe, 1 - mine if e == 1 else mine).start()

    def sum_two(t, stripe, e):
        own_copy(t, stripe, e).wait()
        one_copy(t, stripe, e).wait_recv()
        return own[t][stripe][e].astype(F32) + first_in[t][stripe][e].astype(F32)

    def middle(t):
        if t < chunks:
            for stripe in range(2):
                mid[t][stripe][...] = sum_two(t, stripe, 1 - digits[1 - stripe]).astype(BF16)
                two_copy(t, stripe).start()
            start_one(t + 2)

    int_copies = [
        pltpu.make_async_copy(ref.at[pl.ds(pole * blocks, blocks)], row.at[0], int_sem.at[i])
        for i, (ref, row) in enumerate(((node_hbm, node_ref), (slot_hbm, slot_ref)))
    ]
    dv_copy = pltpu.make_async_copy(deriv, dv, dv_sem)

    barrier = pltpu.get_barrier_semaphore()
    for r in range(1, poles):
        pl.semaphore_signal(
            barrier, inc=1, device_id={"pole": (pole + r) % poles}, device_id_type=MESH
        )

    @pl.loop(1, nodes)
    def _(k):
        pl.semaphore_signal(
            barrier, inc=1, device_id={"node": (node + k) % nodes}, device_id_type=MESH
        )

    for copy in int_copies:
        copy.start()
    for t in range(chunks):
        for stripe in range(2):
            for e in range(2):
                own_copy(t, stripe, e).start()
    dv_copy.start()
    pl.semaphore_wait(barrier, poles - 1 + nodes - 1)

    start_one(0)
    start_one(1)

    for copy in int_copies:
        copy.wait()
    dest_row = node_ref[...]
    slot_row = slot_ref[...]
    hot = dest_row == iota((nodes, blocks), 0)
    before = onehot(iota((blocks, blocks), 0) < iota((blocks, blocks), 1))
    rank = jnp.dot(onehot(hot), before, preferred_element_type=F32)
    ranks[...] = jnp.where(hot, rank, -1.0)
    digit_high = (slot_row // DIGIT + 1).astype(F32)
    digit_low = (slot_row % DIGIT).astype(F32)
    which = iota((ROWS, blocks), 0)
    slot_rows[...] = jnp.where(
        which == 0, digit_high, jnp.where(which == 1, digit_low, 0.0)
    ).astype(BF16)

    def slot_copy(k):
        return pltpu.make_async_remote_copy(
            src_ref=slot_send.at[k],
            dst_ref=slot_recv.at[k],
            send_sem=sl_send.at[k],
            recv_sem=sl_recv.at[k],
            device_id={"node": (node + k) % nodes},
            device_id_type=MESH,
        )

    def make_pack(k):
        row = ranks[pl.ds((node + k) % nodes, 1), :]
        pack[k] = onehot(row == iota((cap, blocks), 0).astype(F32))
        return lax.dot_general(slot_rows[...], pack[k], NT, preferred_element_type=F32)

    @pl.loop(1, nodes)
    def _(k):
        slot_send[k] = make_pack(k)
        slot_copy(k).start()

    slot_recv[0] = make_pack(0)

    dv_copy.wait()
    wide = chunks * CHUNK
    for c in range(3):
        for start, first, sign in ((c * half, 0, 1.0), ((3 + c) * half, half, -1.0)):
            low = start // LANES * LANES
            high = min(-(-(start + half) // LANES) * LANES, total)
            src = iota((wide, high - low), 1) + (low - start)
            row = iota((wide, high - low), 0) - first
            moved = jnp.where((src == row) & (row >= 0) & (row < half), sign, 0.0).astype(BF16)
            piece = jnp.dot(moved, dv[low:high, :], preferred_element_type=F32)
            got = piece if first == 0 else got + piece
        aligned[c] = got.astype(BF16)

    def ex_copy(t, k):
        return pltpu.make_async_remote_copy(
            src_ref=send_buf[t].at[k],
            dst_ref=recv_buf[t].at[k],
            send_sem=ex_send.at[t, k],
            recv_sem=ex_recv.at[t, k],
            device_id={"node": (node + k) % nodes},
            device_id_type=MESH,
        )

    def exchange(t):
        for stripe in range(2):
            start, size = stripe_rows(t, stripe)
            summed = sum_two(t, stripe, digits[1 - stripe])
            two_copy(t, stripe).wait_recv()
            summed = summed + second_in[t][stripe][...].astype(F32)
            density[t][start:start + size, :] = summed.astype(BF16)

        def packed(k):
            return lax.dot_general(
                density[t][...], pack[k], NT, preferred_element_type=F32
            ).astype(BF16)

        @pl.loop(0, nodes - 1)
        def _(i):
            k = near_first(i)
            send_buf[t][k] = packed(k)
            ex_copy(t, k).start()

        recv_buf[t][0] = packed(0)

    def make_place(k):
        pair = slot_recv[k]
        slot = (pair[0:1, :] - 1.0) * DIGIT + pair[1:2, :]
        place[k] = onehot(slot == iota((blocks, cap), 0).astype(F32))

    def contract(t):
        def placed(k):
            return lax.dot_general(
                recv_buf[t][k], place[k], NT, preferred_element_type=F32
            )

        acc[t][...] = placed(0)

        @pl.loop(0, nodes - 1)
        def _(i):
            k = near_first(nodes - 2 - i)
            ex_copy(t, k).wait_recv()
            acc[t][...] += placed(k)

        sums = jnp.zeros((ROWS, blocks), F32)
        for c in range(3):
            prod = acc[t][...] * aligned[c, t * CHUNK:t * CHUNK + rows(t), :].astype(F32)
            sums = jnp.where(which % PART == c, jnp.sum(prod, axis=0, keepdims=True), sums)
        return sums

    middle(0)
    middle(1)
    exchange(0)
    make_place(0)

    @pl.loop(1, nodes)
    def _(k):
        slot_copy(k).wait_recv()
        make_place(k)

    term = jnp.zeros((ROWS, blocks), F32)
    for t in range(1, chunks):
        middle(t + 1)
        exchange(t)
        if t >= 3:
            term = term + contract(t - 3)
    for t in range(max(0, chunks - 3), chunks):
        term = term + contract(t)

    owners = poles * nodes
    group = min(owners, 32)
    height = group * PART
    pieces = split_two(2.0 * term)
    for g in range(owners // group):
        block = iota((height, blocks), 0) // PART + g * group
        owner = (block % poles) * nodes + block // poles
        result = None
        for end in range(2):
            atom = atoms[end:end + 1, :]
            low = onehot(atom % LANES == iota((LANES, blocks), 0))
            here = (atom // LANES) == owner
            for piece in pieces:
                value = jnp.tile(piece.astype(F32), (group // 2, 1))
                lhs = jnp.where(here, value if end == 1 else -value, 0.0).astype(BF16)
                got = lax.dot_general(lhs, low, NT, preferred_element_type=F32)
                result = got if result is None else result + got
        span = group // poles
        force[g * span:(g + 1) * span] = result.reshape(span, poles // 2, ROWS, LANES)

    def fa_copy(k):
        dest = (node + k) % nodes
        return pltpu.make_async_remote_copy(
            src_ref=force.at[dest],
            dst_ref=force_in.at[k],
            send_sem=fa_send.at[k],
            recv_sem=fa_recv.at[k],
            device_id={"node": dest},
            device_id_type=MESH,
        )

    @pl.loop(0, nodes - 1)
    def _(i):
        fa_copy(near_first(i)).start()

    force_two[...] = force[node]

    @pl.loop(0, nodes - 1)
    def _(i):
        k = near_first(nodes - 2 - i)
        fa_copy(k).wait_recv()
        force_two[...] += force_in[k]

    def fb_copy(r):
        dest = (pole + r) % poles
        return pltpu.make_async_remote_copy(
            src_ref=force_two.at[dest // 2],
            dst_ref=force_last.at[r],
            send_sem=fb_send.at[r],
            recv_sem=fb_recv.at[r],
            device_id={"pole": dest},
            device_id_type=MESH,
        )

    for r in range(1, poles):
        fb_copy(r).start()
    final = force_two[pole // 2]
    for r in range(1, poles):
        fb_copy(r).wait_recv()
        final = final + force_last[r]
    out[...] = jnp.where(pole % 2 == 0, final[0:3, :], final[PART:PART + 3, :])

    for t in range(chunks):
        for stripe in range(2):
            two_copy(t, stripe).wait_send()
            for e in range(2):
                one_copy(t, stripe, e).wait_send()

        @pl.loop(1, nodes)
        def _(k):
            ex_copy(t, k).wait_send()

    @pl.loop(1, nodes)
    def _(k):
        slot_copy(k).wait_send()
        fa_copy(k).wait_send()

    for r in range(1, poles):
        fb_copy(r).wait_send()


def body(dens_part, dest_node, pair_slot, deriv, pair_atoms):
    blocks = deriv.shape[0]
    total = deriv.shape[1]
    width = dens_part.shape[2]
    nodes = lax.axis_size("node")
    poles = lax.axis_size("pole")
    cap = 2 * blocks // nodes
    chunks = -(-width // CHUNK)
    sizes = [min(CHUNK, width - t * CHUNK) for t in range(chunks)]
    stripes = [(n // 2 // 16 * 16, n - n // 2 // 16 * 16) for n in sizes]
    dma = pltpu.SemaphoreType.DMA
    vmem = pl.BlockSpec(memory_space=pltpu.VMEM)
    hbm = pl.BlockSpec(memory_space=pl.ANY)
    return pl.pallas_call(
        functools.partial(kernel, poles, nodes, blocks, width, cap),
        out_shape=jax.ShapeDtypeStruct((3, LANES), F32),
        in_specs=[hbm, hbm, hbm, hbm, vmem],
        out_specs=vmem,
        scratch_shapes=[
            [[pltpu.VMEM((2, n, blocks), BF16) for n in pair] for pair in stripes],
            [[pltpu.VMEM((2, n, blocks), BF16) for n in pair] for pair in stripes],
            [[pltpu.VMEM((n, blocks), BF16) for n in pair] for pair in stripes],
            [[pltpu.VMEM((n, blocks), BF16) for n in pair] for pair in stripes],
            pltpu.VMEM((total, blocks), BF16),
            pltpu.VMEM((3, chunks * CHUNK, blocks), BF16),
            pltpu.VMEM((nodes, cap, blocks), BF16),
            pltpu.VMEM((nodes, blocks, cap), BF16),
            pltpu.VMEM((nodes, blocks), F32),
            pltpu.VMEM((ROWS, blocks), BF16),
            pltpu.VMEM((nodes, ROWS, cap), F32),
            pltpu.VMEM((nodes, ROWS, cap), F32),
            [pltpu.VMEM((nodes, n, cap), BF16) for n in sizes],
            [pltpu.VMEM((nodes, n, cap), BF16) for n in sizes],
            [pltpu.VMEM((n, blocks), BF16) for n in sizes],
            [pltpu.VMEM((n, blocks), F32) for n in sizes],
            pltpu.VMEM((nodes, poles // 2, ROWS, LANES), F32),
            pltpu.VMEM((nodes, poles // 2, ROWS, LANES), F32),
            pltpu.VMEM((poles // 2, ROWS, LANES), F32),
            pltpu.VMEM((poles, ROWS, LANES), F32),
            dma((chunks, 2, 2)),
            dma,
            dma((chunks, 2, 2)),
            dma((chunks, 2, 2)),
            dma((chunks, 2)),
            dma((chunks, 2)),
            dma((nodes,)),
            dma((nodes,)),
            dma((chunks, nodes)),
            dma((chunks, nodes)),
            dma((nodes,)),
            dma((nodes,)),
            dma((poles,)),
            dma((poles,)),
            pltpu.VMEM((1, blocks), jnp.int32),
            pltpu.VMEM((1, blocks), jnp.int32),
            dma((2,)),
        ],
        compiler_params=pltpu.CompilerParams(
            collective_id=0, has_side_effects=True, vmem_limit_bytes=60 << 20
        ),
    )(
        dens_part[0].T,
        dest_node,
        pair_slot,
        deriv.T,
        pair_atoms,
    )


def solution(mesh):
    return jax.shard_map(
        body,
        mesh=mesh,
        in_specs=(
            P("pole", "node", None),
            P("node"),
            P("node"),
            P(("pole", "node"), None),
            P(None, ("pole", "node")),
        ),
        out_specs=P(None, ("pole", "node")),
        check_vma=False,
    )
```

```python
import functools

import jax
import jax.numpy as jnp
from jax import lax
from jax.experimental import pallas as pl
from jax.experimental.pallas import tpu as pltpu
from jax.sharding import PartitionSpec as P

LANES = 128
CHUNK = 96
ROWS = 8
DIGIT = 32
PART = 4
MESH = pl.DeviceIdType.MESH
NT = (((1,), (1,)), ((), ()))
F32 = jnp.float32
BF16 = jnp.bfloat16


def iota(shape, dim):
    return lax.broadcasted_iota(jnp.int32, shape, dim)


def onehot(cond):
    return jnp.where(cond, 1.0, 0.0).astype(BF16)


def split_two(x):
    high = x.astype(BF16)
    return high, (x - high.astype(F32)).astype(BF16)


def kernel(
    poles, nodes, blocks, width, cap,
    dens, node_hbm, slot_hbm, deriv, atoms, out,
    own, parts, dv, aligned, pack, place, ranks, slot_rows, slot_send, slot_recv,
    send_buf, recv_buf, density, acc, force, force_in, force_two, force_last,
    own_sem, dv_sem, rs_send, rs_recv, sl_send, sl_recv, ex_send, ex_recv,
    fa_send, fa_recv, fb_send, fb_recv, node_ref, slot_ref, int_sem,
):
    half = width // 2
    chunks = -(-width // CHUNK)
    total = deriv.shape[0]
    pole = lax.axis_index("pole")
    node = lax.axis_index("node")

    def near_first(i):
        return nodes // 2 + (1 - 2 * (i % 2)) * ((i + 1) // 2)

    def rows(t):
        return min(CHUNK, width - t * CHUNK)

    own_copies = []
    for t in range(chunks):
        copy = pltpu.make_async_copy(
            dens.at[pl.ds(t * CHUNK, rows(t)), pl.ds(pole * blocks, blocks)],
            own[t],
            own_sem.at[t],
        )
        own_copies.append(copy)
    int_copies = [
        pltpu.make_async_copy(ref.at[pl.ds(pole * blocks, blocks)], row.at[0], int_sem.at[i])
        for i, (ref, row) in enumerate(((node_hbm, node_ref), (slot_hbm, slot_ref)))
    ]
    dv_copy = pltpu.make_async_copy(deriv, dv, dv_sem)

    barrier = pltpu.get_barrier_semaphore()
    for r in range(1, poles):
        pl.semaphore_signal(
            barrier, inc=1, device_id={"pole": (pole + r) % poles}, device_id_type=MESH
        )

    @pl.loop(1, nodes)
    def _(k):
        pl.semaphore_signal(
            barrier, inc=1, device_id={"node": (node + k) % nodes}, device_id_type=MESH
        )

    for copy in int_copies + own_copies:
        copy.start()
    dv_copy.start()
    pl.semaphore_wait(barrier, poles - 1 + nodes - 1)

    def rs_copy(t, r):
        dest = (pole + r) % poles
        return pltpu.make_async_remote_copy(
            src_ref=dens.at[pl.ds(t * CHUNK, rows(t)), pl.ds(dest * blocks, blocks)],
            dst_ref=parts[t].at[r - 1],
            send_sem=rs_send.at[t, r - 1],
            recv_sem=rs_recv.at[t, r - 1],
            device_id={"pole": dest},
            device_id_type=MESH,
        )

    for t in range(chunks):
        for r in range(1, poles):
            rs_copy(t, r).start()

    for copy in int_copies:
        copy.wait()
    dest_row = node_ref[...]
    slot_row = slot_ref[...]
    hot = dest_row == iota((nodes, blocks), 0)
    before = onehot(iota((blocks, blocks), 0) < iota((blocks, blocks), 1))
    rank = jnp.dot(onehot(hot), before, preferred_element_type=F32)
    ranks[...] = jnp.where(hot, rank, -1.0)
    digit_high = (slot_row // DIGIT + 1).astype(F32)
    digit_low = (slot_row % DIGIT).astype(F32)
    which = iota((ROWS, blocks), 0)
    slot_rows[...] = jnp.where(
        which == 0, digit_high, jnp.where(which == 1, digit_low, 0.0)
    ).astype(BF16)

    def slot_copy(k):
        return pltpu.make_async_remote_copy(
            src_ref=slot_send.at[k],
            dst_ref=slot_recv.at[k],
            send_sem=sl_send.at[k],
            recv_sem=sl_recv.at[k],
            device_id={"node": (node + k) % nodes},
            device_id_type=MESH,
        )

    def make_pack(k):
        row = ranks[pl.ds((node + k) % nodes, 1), :]
        pack[k] = onehot(row == iota((cap, blocks), 0).astype(F32))
        return lax.dot_general(slot_rows[...], pack[k], NT, preferred_element_type=F32)

    @pl.loop(1, nodes)
    def _(k):
        slot_send[k] = make_pack(k)
        slot_copy(k).start()

    slot_recv[0] = make_pack(0)

    dv_copy.wait()
    wide = chunks * CHUNK
    for c in range(3):
        for start, first, sign in ((c * half, 0, 1.0), ((3 + c) * half, half, -1.0)):
            low = start // LANES * LANES
            high = min(-(-(start + half) // LANES) * LANES, total)
            src = iota((wide, high - low), 1) + (low - start)
            row = iota((wide, high - low), 0) - first
            moved = jnp.where((src == row) & (row >= 0) & (row < half), sign, 0.0).astype(BF16)
            piece = jnp.dot(moved, dv[low:high, :], preferred_element_type=F32)
            got = piece if first == 0 else got + piece
        aligned[c] = got.astype(BF16)

    def ex_copy(t, k):
        return pltpu.make_async_remote_copy(
            src_ref=send_buf[t].at[k],
            dst_ref=recv_buf[t].at[k],
            send_sem=ex_send.at[t, k],
            recv_sem=ex_recv.at[t, k],
            device_id={"node": (node + k) % nodes},
            device_id_type=MESH,
        )

    def exchange(t):
        own_copies[t].wait()
        for r in range(1, poles):
            rs_copy(t, r).wait_recv()
        summed = own[t][...].astype(F32)
        for r in range(1, poles):
            summed = summed + parts[t][r - 1].astype(F32)
        density[t][...] = summed.astype(BF16)

        def packed(k):
            return lax.dot_general(
                density[t][...], pack[k], NT, preferred_element_type=F32
            ).astype(BF16)

        @pl.loop(0, nodes - 1)
        def _(i):
            k = near_first(i)
            send_buf[t][k] = packed(k)
            ex_copy(t, k).start()

        recv_buf[t][0] = packed(0)

    def make_place(k):
        digits = slot_recv[k]
        slot = (digits[0:1, :] - 1.0) * DIGIT + digits[1:2, :]
        place[k] = onehot(slot == iota((blocks, cap), 0).astype(F32))

    def contract(t):
        def placed(k):
            return lax.dot_general(
                recv_buf[t][k], place[k], NT, preferred_element_type=F32
            )

        acc[t][...] = placed(0)

        @pl.loop(0, nodes - 1)
        def _(i):
            k = near_first(nodes - 2 - i)
            ex_copy(t, k).wait_recv()
            acc[t][...] += placed(k)

        sums = jnp.zeros((ROWS, blocks), F32)
        for c in range(3):
            prod = acc[t][...] * aligned[c, t * CHUNK:t * CHUNK + rows(t), :].astype(F32)
            sums = jnp.where(which % PART == c, jnp.sum(prod, axis=0, keepdims=True), sums)
        return sums

    exchange(0)
    make_place(0)

    @pl.loop(1, nodes)
    def _(k):
        slot_copy(k).wait_recv()
        make_place(k)

    term = jnp.zeros((ROWS, blocks), F32)
    for t in range(1, chunks):
        exchange(t)
        if t >= 3:
            term = term + contract(t - 3)
    for t in range(max(0, chunks - 3), chunks):
        term = term + contract(t)

    owners = poles * nodes
    group = min(owners, 32)
    height = group * PART
    pieces = split_two(2.0 * term)
    for g in range(owners // group):
        block = iota((height, blocks), 0) // PART + g * group
        owner = (block % poles) * nodes + block // poles
        result = None
        for end in range(2):
            atom = atoms[end:end + 1, :]
            low = onehot(atom % LANES == iota((LANES, blocks), 0))
            here = (atom // LANES) == owner
            for piece in pieces:
                value = jnp.tile(piece.astype(F32), (group // 2, 1))
                lhs = jnp.where(here, value if end == 1 else -value, 0.0).astype(BF16)
                got = lax.dot_general(lhs, low, NT, preferred_element_type=F32)
                result = got if result is None else result + got
        span = group // poles
        force[g * span:(g + 1) * span] = result.reshape(span, poles // 2, ROWS, LANES)

    def fa_copy(k):
        dest = (node + k) % nodes
        return pltpu.make_async_remote_copy(
            src_ref=force.at[dest],
            dst_ref=force_in.at[k],
            send_sem=fa_send.at[k],
            recv_sem=fa_recv.at[k],
            device_id={"node": dest},
            device_id_type=MESH,
        )

    @pl.loop(0, nodes - 1)
    def _(i):
        fa_copy(near_first(i)).start()

    force_two[...] = force[node]

    @pl.loop(0, nodes - 1)
    def _(i):
        k = near_first(nodes - 2 - i)
        fa_copy(k).wait_recv()
        force_two[...] += force_in[k]

    def fb_copy(r):
        dest = (pole + r) % poles
        return pltpu.make_async_remote_copy(
            src_ref=force_two.at[dest // 2],
            dst_ref=force_last.at[r],
            send_sem=fb_send.at[r],
            recv_sem=fb_recv.at[r],
            device_id={"pole": dest},
            device_id_type=MESH,
        )

    for r in range(1, poles):
        fb_copy(r).start()
    final = force_two[pole // 2]
    for r in range(1, poles):
        fb_copy(r).wait_recv()
        final = final + force_last[r]
    out[...] = jnp.where(pole % 2 == 0, final[0:3, :], final[PART:PART + 3, :])

    for t in range(chunks):
        for r in range(1, poles):
            rs_copy(t, r).wait_send()

        @pl.loop(1, nodes)
        def _(k):
            ex_copy(t, k).wait_send()

    @pl.loop(1, nodes)
    def _(k):
        slot_copy(k).wait_send()
        fa_copy(k).wait_send()

    for r in range(1, poles):
        fb_copy(r).wait_send()


def body(dens_part, dest_node, pair_slot, deriv, pair_atoms):
    blocks = deriv.shape[0]
    total = deriv.shape[1]
    width = dens_part.shape[2]
    nodes = lax.axis_size("node")
    poles = lax.axis_size("pole")
    cap = 2 * blocks // nodes
    chunks = -(-width // CHUNK)
    sizes = [min(CHUNK, width - t * CHUNK) for t in range(chunks)]
    dma = pltpu.SemaphoreType.DMA
    vmem = pl.BlockSpec(memory_space=pltpu.VMEM)
    hbm = pl.BlockSpec(memory_space=pl.ANY)
    return pl.pallas_call(
        functools.partial(kernel, poles, nodes, blocks, width, cap),
        out_shape=jax.ShapeDtypeStruct((3, LANES), F32),
        in_specs=[hbm, hbm, hbm, hbm, vmem],
        out_specs=vmem,
        scratch_shapes=[
            [pltpu.VMEM((n, blocks), BF16) for n in sizes],
            [pltpu.VMEM((poles - 1, n, blocks), BF16) for n in sizes],
            pltpu.VMEM((total, blocks), BF16),
            pltpu.VMEM((3, chunks * CHUNK, blocks), BF16),
            pltpu.VMEM((nodes, cap, blocks), BF16),
            pltpu.VMEM((nodes, blocks, cap), BF16),
            pltpu.VMEM((nodes, blocks), F32),
            pltpu.VMEM((ROWS, blocks), BF16),
            pltpu.VMEM((nodes, ROWS, cap), F32),
            pltpu.VMEM((nodes, ROWS, cap), F32),
            [pltpu.VMEM((nodes, n, cap), BF16) for n in sizes],
            [pltpu.VMEM((nodes, n, cap), BF16) for n in sizes],
            [pltpu.VMEM((n, blocks), BF16) for n in sizes],
            [pltpu.VMEM((n, blocks), F32) for n in sizes],
            pltpu.VMEM((nodes, poles // 2, ROWS, LANES), F32),
            pltpu.VMEM((nodes, poles // 2, ROWS, LANES), F32),
            pltpu.VMEM((poles // 2, ROWS, LANES), F32),
            pltpu.VMEM((poles, ROWS, LANES), F32),
            dma((chunks,)),
            dma,
            dma((chunks, poles - 1)),
            dma((chunks, poles - 1)),
            dma((nodes,)),
            dma((nodes,)),
            dma((chunks, nodes)),
            dma((chunks, nodes)),
            dma((nodes,)),
            dma((nodes,)),
            dma((poles,)),
            dma((poles,)),
            pltpu.VMEM((1, blocks), jnp.int32),
            pltpu.VMEM((1, blocks), jnp.int32),
            dma((2,)),
        ],
        compiler_params=pltpu.CompilerParams(
            collective_id=0, has_side_effects=True, vmem_limit_bytes=60 << 20
        ),
    )(
        dens_part[0].T,
        dest_node,
        pair_slot,
        deriv.T,
        pair_atoms,
    )


def solution(mesh):
    return jax.shard_map(
        body,
        mesh=mesh,
        in_specs=(
            P("pole", "node", None),
            P("node"),
            P("node"),
            P(("pole", "node"), None),
            P(None, ("pole", "node")),
        ),
        out_specs=P(None, ("pole", "node")),
        check_vma=False,
    )
```
